32 devices in a mesh: ctx: 8 (over z, x), head: 4 (over y, core).
Axes of the slice: x: 2, y: 2, z: 4, core: 2. Of those that a mesh axis runs over, the one named last changes fastest.
Arguments:
- query: bfloat16 [8192, 32, 128], P('ctx', 'head'), may hold values from -6 to 6
- keys: bfloat16 [8192, 8, 128], P('ctx', 'head'), may hold values from -6 to 6
- values: bfloat16 [8192, 8, 128], P('ctx', 'head'), may hold values from -6 to 6
- attn_out: bfloat16 [8192, 32, 128], P('ctx', 'head'), may hold values from -6 to 6
- output_gradient: bfloat16 [8192, 32, 128], P('ctx', 'head'), may hold values from -6 to 6
- lse: float32 [32, 8192], P('head', 'ctx'), may hold values from 4 to 6
- doc_offsets: int32 [9], replicated, may hold values from 0 to 8192, as said below
- tile_first: int32 [8], replicated, may hold values from 0 to 56, as said below
Outputs:
- grad_query: bfloat16 [8192, 32, 128], P(('ctx', 'head'))
- grad_keys: bfloat16 [8192, 8, 128], P(('ctx', 'head'))
- grad_values: bfloat16 [8192, 8, 128], P(('ctx', 'head'))
The draws below stay inside these ranges and needn't reach their ends.
Inputs may be any that keep to these rules, and one draw needn't show every extreme that they name: doc_offsets[0] = 0, doc_offsets[8] = 8192, strictly rising; document d holds tokens doc_offsets[d] to doc_offsets[d + 1] - 1. tile_first[i] = max(start of the document that holds token i * 1024, i * 1024 - 4095) // 128.
All inputs are finite; a program needn't handle non-finite values.
Results may differ from the reference program's by a relative error of at most 0.0055.
Values may be sent and summed in bfloat16 or wider, within the bound.
No kernel may reach another device: no remote copies, remote signals or barrier semaphores. Data moves between devices by JAX's collectives and lax.ppermute only.
A program may use at most 192 MiB of HBM per device.

```python
import math
import jax
import jax.numpy as jnp
from jax import lax

QUERY_HEAD_COUNT = 32
KEY_VALUE_HEADS = 8
HEAD_SIZE = 128
LOOKBACK_TOKENS = 4096
TILE = 128
TOK_DEV = 1024
DOCS = 8
PACKED_TOKENS = 8192


def document_offsets(key):
    folded = jax.random.fold_in(key, 11)
    shuffled = jax.random.permutation(folded, PACKED_TOKENS - 1)[:DOCS - 1] + 1
    cut_points = jnp.sort(shuffled).astype(jnp.int32)
    return jnp.concatenate([jnp.zeros((1,), jnp.int32), cut_points, jnp.full((1,), PACKED_TOKENS, jnp.int32)])


def draw_doc_offsets(key, part):
    return document_offsets(key)


def draw_tile_first(key, part):
    bounds = document_offsets(key)
    shard_start = jnp.arange(PACKED_TOKENS // TOK_DEV, dtype=jnp.int32) * TOK_DEV
    holder = jnp.sum((shard_start[:, None] >= bounds[None, 1:-1]).astype(jnp.int32), axis=1)
    doc_start = jnp.take(bounds, holder)
    first_needed = jnp.maximum(doc_start, shard_start - LOOKBACK_TOKENS + 1)
    return (first_needed // TILE).astype(jnp.int32)


def block_levels(key, shape, shards, low, largest):
    gain, own = 1.0, jax.random.fold_in(key, 6)
    for dim, shards_of in shards:
        heights = jnp.exp(jax.random.uniform(jax.random.fold_in(own, dim), (shards_of,), jnp.float32, low / len(shards), largest / len(shards)))
        gain = gain * jnp.repeat(heights, shape[dim] // shards_of).reshape([-1 if axis == dim else 1 for axis in range(len(shape))])
    return gain


def normal_values(own_key, extent, width, most, split=(), kind=jnp.bfloat16):
    array = width * jax.random.normal(own_key, extent, jnp.float32)
    if split:
        array = array * block_levels(own_key, extent, split, -0.22, 0.18)
    return jnp.clip(array, -most, most).astype(kind)


def setup_inputs(seed: int = 0) -> dict:
    key_of = jax.random.split(jax.random.key(seed), 9)
    query = normal_values(key_of[0], (PACKED_TOKENS, QUERY_HEAD_COUNT, HEAD_SIZE), 1.0, 6.0, ((0, 8), (1, 4)))
    keys = normal_values(key_of[1], (PACKED_TOKENS, KEY_VALUE_HEADS, HEAD_SIZE), 1.0, 6.0, ((0, 8), (1, 4)))
    values = normal_values(key_of[2], (PACKED_TOKENS, KEY_VALUE_HEADS, HEAD_SIZE), 1.0, 6.0, ((0, 8), (1, 4)))
    attn_out = normal_values(key_of[3], (PACKED_TOKENS, QUERY_HEAD_COUNT, HEAD_SIZE), 1.0, 6.0, ((0, 8), (1, 4)))
    output_gradient = normal_values(key_of[4], (PACKED_TOKENS, QUERY_HEAD_COUNT, HEAD_SIZE), 1.0, 6.0, ((0, 8), (1, 4)))
    lse = jnp.clip(4.0 + 2.0 * jax.random.uniform(key_of[5], (QUERY_HEAD_COUNT, PACKED_TOKENS), jnp.float32) ** block_levels(key_of[5], (QUERY_HEAD_COUNT, PACKED_TOKENS), ((0, 4), (1, 8)), -0.2, 0.2), 4.0, 6.0)
    doc_offsets = draw_doc_offsets(jax.random.fold_in(key_of[8], 71), 0)
    tile_first = draw_tile_first(jax.random.fold_in(key_of[8], 71), 0)
    return {"query": query, "keys": keys, "values": values, "attn_out": attn_out, "output_gradient": output_gradient, "lse": lse, "doc_offsets": doc_offsets, "tile_first": tile_first}


def document_ids(positions, doc_offsets):
    cut_points = doc_offsets[1:-1]
    return lax.optimization_barrier(jnp.sum((positions[:, None] >= cut_points[None, :]).astype(jnp.int32), axis=1))

def visibility(query_pos, key_pos, doc_offsets, first_key):
    same_doc = document_ids(query_pos, doc_offsets)[:, None] == document_ids(key_pos, doc_offsets)[None, :]
    distance = query_pos[:, None] - key_pos[None, :]
    listed = key_pos[None, :] >= first_key[:, None]
    return same_doc & (distance >= 0) & (distance < LOOKBACK_TOKENS) & listed

def diagonal_band_terms(block_query_rows, block_output_gradient, block_logsumexp, block_delta_rows, block_key_rows, block_value_rows, visible_mask, logit_scale_factor):
    widened_rows = jnp.float32
    scores = jnp.einsum('qhgd,khd->hgqk', block_query_rows.astype(widened_rows), block_key_rows.astype(widened_rows)) * logit_scale_factor
    weights = jnp.where(visible_mask[None, None], jnp.exp(scores - block_logsumexp[..., None]), 0.0)
    weights_b = weights.astype(jnp.bfloat16)
    partial_value_gradient = jnp.einsum('hgqk,qhgd->khd', weights_b.astype(widened_rows), block_output_gradient.astype(widened_rows))
    grad_weights = jnp.einsum('qhgd,khd->hgqk', block_output_gradient.astype(widened_rows), block_value_rows.astype(widened_rows))
    grad_scores = (weights * (grad_weights - block_delta_rows[..., None])).astype(jnp.bfloat16)
    partial_query_gradient = jnp.einsum('hgqk,khd->qhgd', grad_scores.astype(widened_rows), block_key_rows.astype(widened_rows))
    partial_key_gradient = jnp.einsum('hgqk,qhgd->khd', grad_scores.astype(widened_rows), block_query_rows.astype(widened_rows))
    return (partial_query_gradient, partial_key_gradient, partial_value_gradient)

def reference(query, keys, values, attn_out, output_gradient, lse, doc_offsets, tile_first):
    tile_block = min(512, TOK_DEV)
    queries_per_group = QUERY_HEAD_COUNT // KEY_VALUE_HEADS
    logit_scale_factor = 1.0 / math.sqrt(HEAD_SIZE)
    widened_rows = jnp.float32
    delta_values = lax.optimization_barrier(jnp.sum(output_gradient.astype(widened_rows) * attn_out.astype(widened_rows), axis=-1)).T
    padding_rows = jnp.zeros((LOOKBACK_TOKENS, KEY_VALUE_HEADS, HEAD_SIZE), keys.dtype)
    keys_padded = jnp.concatenate([padding_rows, keys], axis=0)
    values_padded = jnp.concatenate([padding_rows, values], axis=0)
    zero_sum_init = jnp.zeros((LOOKBACK_TOKENS + PACKED_TOKENS, KEY_VALUE_HEADS, HEAD_SIZE), widened_rows)

    def query_step(totals, block_index):
        sums_k, sums_v = totals
        first_row_index = block_index * tile_block
        query_pos = first_row_index + jnp.arange(tile_block, dtype=jnp.int32)
        first_key = jnp.take(tile_first, query_pos // TOK_DEV) * TILE
        block_query_rows = lax.dynamic_slice_in_dim(query, first_row_index, tile_block, 0).reshape(tile_block, KEY_VALUE_HEADS, queries_per_group, HEAD_SIZE)
        block_output_gradient = lax.dynamic_slice_in_dim(output_gradient, first_row_index, tile_block, 0).reshape(tile_block, KEY_VALUE_HEADS, queries_per_group, HEAD_SIZE)
        block_logsumexp = lax.dynamic_slice_in_dim(lse, first_row_index, tile_block, 1).reshape(KEY_VALUE_HEADS, queries_per_group, tile_block)
        block_delta_rows = lax.dynamic_slice_in_dim(delta_values, first_row_index, tile_block, 1).reshape(KEY_VALUE_HEADS, queries_per_group, tile_block)
        query_gradient_sums = jnp.zeros((tile_block, KEY_VALUE_HEADS, queries_per_group, HEAD_SIZE), widened_rows)
        for section in range(LOOKBACK_TOKENS // tile_block + 1):
            key_start = first_row_index + section * tile_block
            key_pos = key_start - LOOKBACK_TOKENS + jnp.arange(tile_block, dtype=jnp.int32)
            visible_mask = visibility(query_pos, key_pos, doc_offsets, first_key)
            block_key_rows = lax.dynamic_slice_in_dim(keys_padded, key_start, tile_block, 0)
            block_value_rows = lax.dynamic_slice_in_dim(values_padded, key_start, tile_block, 0)
            partial_query_gradient, partial_key_gradient, partial_value_gradient = lax.cond(jnp.any(visible_mask), lambda: diagonal_band_terms(block_query_rows, block_output_gradient, block_logsumexp, block_delta_rows, block_key_rows, block_value_rows, visible_mask, logit_scale_factor), lambda: (jnp.zeros((tile_block, KEY_VALUE_HEADS, queries_per_group, HEAD_SIZE), widened_rows), jnp.zeros((tile_block, KEY_VALUE_HEADS, HEAD_SIZE), widened_rows), jnp.zeros((tile_block, KEY_VALUE_HEADS, HEAD_SIZE), widened_rows)))
            query_gradient_sums = query_gradient_sums + partial_query_gradient
            sums_k = lax.dynamic_update_slice_in_dim(sums_k, lax.dynamic_slice_in_dim(sums_k, key_start, tile_block, 0) + partial_key_gradient, key_start, 0)
            sums_v = lax.dynamic_update_slice_in_dim(sums_v, lax.dynamic_slice_in_dim(sums_v, key_start, tile_block, 0) + partial_value_gradient, key_start, 0)
        return ((sums_k, sums_v), query_gradient_sums.reshape(tile_block, QUERY_HEAD_COUNT, HEAD_SIZE))
    (sums_k, sums_v), query_gradient_sums = lax.scan(query_step, (zero_sum_init, zero_sum_init), jnp.arange(PACKED_TOKENS // tile_block, dtype=jnp.int32))
    grad_query = (query_gradient_sums.reshape(PACKED_TOKENS, QUERY_HEAD_COUNT, HEAD_SIZE) * logit_scale_factor).astype(jnp.bfloat16)
    grad_keys = (sums_k[LOOKBACK_TOKENS:] * logit_scale_factor).astype(jnp.bfloat16)
    grad_values = sums_v[LOOKBACK_TOKENS:].astype(jnp.bfloat16)
    return (grad_query, grad_keys, grad_values)
```

```python
import functools
import math

import jax
import jax.numpy as jnp
from jax import lax
from jax.experimental import pallas as pl
from jax.experimental.pallas import tpu as pltpu
from jax.sharding import PartitionSpec as P

LOOKBACK_TOKENS = 4096
TILE = 128
QUERY_BLOCK = 128
KEY_BLOCK = 256
BUCKET = 512
F32 = jnp.float32
BF16 = jnp.bfloat16
LOG2E = math.log2(math.e)


def dot(a, b, dim_a, dim_b):
    return lax.dot_general(
        a, b, (((dim_a,), (dim_b,)), ((), ())), preferred_element_type=F32
    )


def lower_bound(positions, offsets_ref, floor):
    bound = jnp.maximum(positions - (LOOKBACK_TOKENS - 1), floor)
    for d in range(1, offsets_ref.shape[0] - 1):
        cut = offsets_ref[d]
        bound = jnp.maximum(bound, jnp.where(positions >= cut, cut, 0))
    return bound


def attention_kernel(
    sources, tokens, group, has_partial, last,
    offsets_ref, first_ref, shard_ref, q_ref, do_ref, lse_ref, delta_ref, *rest
):
    count = len(sources)
    kv_refs, rest = rest[:count], rest[count:]
    if has_partial:
        partial_ref, rest = rest[0], rest[1:]
    dq_ref, rest = rest[0], rest[1:]
    dkv_refs, rest = rest[:count], rest[count:]
    (k_all, v_all, kt_all, dk_acc, dv_acc, dq_acc, lo_rows, pos_rows,
     scores, dprobs, work, sems) = rest
    rows = group * QUERY_BLOCK
    blocks = tokens // QUERY_BLOCK
    scale = LOG2E / math.sqrt(q_ref.shape[1])
    shard = shard_ref[0]
    query_start = shard * tokens
    floor = first_ref[shard] * TILE

    starts = []
    total = 0
    for _, _, length in sources:
        starts.append(total)
        total += length
    copies = []
    for index, (_, _, length) in enumerate(sources):
        at = pl.ds(starts[index], length)
        copies.append(pltpu.make_async_copy(kv_refs[index].at[0], k_all.at[at], sems.at[2 * index]))
        copies.append(
            pltpu.make_async_copy(kv_refs[index].at[1], v_all.at[at], sems.at[2 * index + 1])
        )
    for copy in copies:
        copy.start()

    def scalar_bound(position):
        bound = jnp.maximum(position - (LOOKBACK_TOKENS - 1), floor)
        for d in range(1, offsets_ref.shape[0] - 1):
            cut = offsets_ref[d]
            bound = jnp.where(position >= cut, jnp.maximum(bound, cut), bound)
        return bound

    bounds = [scalar_bound(query_start + b * QUERY_BLOCK) for b in range(blocks)]
    lane = lax.broadcasted_iota(jnp.int32, (1, QUERY_BLOCK), 1)
    for b in range(blocks):
        positions = lane + (query_start + b * QUERY_BLOCK)
        bound = lower_bound(positions, offsets_ref, floor)
        for g in range(group):
            at = pl.ds(b * rows + g * QUERY_BLOCK, QUERY_BLOCK)
            lo_rows[:, at] = bound
            pos_rows[:, at] = positions

    filled = jnp.int32(0)
    for (distance, offset, length), start in zip(sources, starts):
        base = (shard - distance) * tokens + offset

        def add_key_block(ik, filled, base=base, start=start):
            key_start = base + ik * KEY_BLOCK
            for b in range(blocks):
                active = (key_start + (KEY_BLOCK - 1) >= bounds[b]) & (
                    key_start <= query_start + (b * QUERY_BLOCK + QUERY_BLOCK - 1)
                )
                work[0, filled] = start + ik * KEY_BLOCK
                work[1, filled] = b * rows
                work[2, filled] = key_start
                filled = filled + active.astype(jnp.int32)
            return filled

        filled = lax.fori_loop(0, length // KEY_BLOCK, add_key_block, filled)
    for extra in range(2):
        work[0, filled + extra] = 0
        work[1, filled + extra] = 0
        work[2, filled + extra] = jnp.int32(1 << 30)

    dk_acc[...] = jnp.zeros_like(dk_acc)
    dv_acc[...] = jnp.zeros_like(dv_acc)
    if has_partial:
        dq_acc[...] = partial_ref[...]
    else:
        dq_acc[...] = jnp.zeros_like(dq_acc)
    for copy in copies:
        copy.wait()
    for at in range(0, total, KEY_BLOCK):
        kt_all[:, pl.ds(at, KEY_BLOCK)] = k_all[pl.ds(at, KEY_BLOCK), :].T

    def place(item):
        key_rows = pl.ds(pl.multiple_of(work[0, item], KEY_BLOCK), KEY_BLOCK)
        query_rows = pl.ds(pl.multiple_of(work[1, item], rows), rows)
        return key_rows, query_rows

    def products(item, slot):
        key_rows, query_rows = place(item)
        scores[slot] = dot(k_all[key_rows, :], q_ref[query_rows, :], 1, 1)
        dprobs[slot] = dot(v_all[key_rows, :], do_ref[query_rows, :], 1, 1)

    def gradients(item, slot):
        key_rows, query_rows = place(item)
        keys = lax.broadcasted_iota(jnp.int32, (KEY_BLOCK, 1), 0) + work[2, item]
        seen = (keys >= lo_rows[:, query_rows]) & (keys <= pos_rows[:, query_rows])
        probs = jnp.where(
            seen, jnp.exp2(scores[slot] * scale - lse_ref[:, query_rows]), 0.0
        )
        dv_acc[key_rows, :] += dot(probs.astype(BF16), do_ref[query_rows, :], 1, 0)
        dscores = (probs * (dprobs[slot] - delta_ref[:, query_rows])).astype(BF16)
        dk_acc[key_rows, :] += dot(dscores, q_ref[query_rows, :], 1, 0)
        dq_acc[:, query_rows] += dot(kt_all[:, key_rows], dscores, 1, 0)

    @pl.when(filled > 0)
    def _():
        products(0, 0)

        def two_items(step, carry):
            item = 2 * step
            products(item + 1, 1)
            gradients(item, 0)
            products(item + 2, 0)
            gradients(item + 1, 1)
            return carry

        lax.fori_loop(0, (filled + 1) // 2, two_items, 0)

    out_scale = 1.0 / math.sqrt(q_ref.shape[1])
    for index, (_, _, length) in enumerate(sources):
        at = pl.ds(starts[index], length)
        dkv_refs[index][0] = (dk_acc[at, :] * out_scale).astype(dkv_refs[index].dtype)
        dkv_refs[index][1] = dv_acc[at, :].astype(dkv_refs[index].dtype)
    if last:
        for at in range(0, blocks * rows, rows):
            dq_ref[pl.ds(at, rows), :] = (dq_acc[:, pl.ds(at, rows)].T * out_scale).astype(BF16)
    else:
        dq_ref[...] = dq_acc[...]


def attend(sources, tokens, group, scalars, q, do, lse, delta, kvs, partial, last):
    total = sum(length for _, _, length in sources)
    rows, size = q.shape
    any_space = pl.BlockSpec(memory_space=pl.ANY)
    vmem = pl.BlockSpec(memory_space=pltpu.VMEM)
    smem = pl.BlockSpec(memory_space=pltpu.SMEM)
    operands = [*scalars, q, do, lse, delta, *kvs]
    specs = [smem] * 3 + [vmem] * 4 + [any_space] * len(kvs)
    if partial is not None:
        operands.append(partial)
        specs.append(vmem)
    dkv_shapes = [
        jax.ShapeDtypeStruct((2, length, size), F32 if distance == 0 else BF16)
        for distance, _, length in sources
    ]
    dq_shape = (
        jax.ShapeDtypeStruct((rows, size), BF16) if last else jax.ShapeDtypeStruct((size, rows), F32)
    )
    pairs = (total // KEY_BLOCK) * (tokens // QUERY_BLOCK)
    item_rows = group * QUERY_BLOCK
    return pl.pallas_call(
        functools.partial(
            attention_kernel, sources, tokens, group, partial is not None, last
        ),
        out_shape=[dq_shape, *dkv_shapes],
        in_specs=specs,
        out_specs=[vmem] * (1 + len(sources)),
        scratch_shapes=[
            pltpu.VMEM((total, size), BF16),
            pltpu.VMEM((total, size), BF16),
            pltpu.VMEM((size, total), BF16),
            pltpu.VMEM((total, size), F32),
            pltpu.VMEM((total, size), F32),
            pltpu.VMEM((size, rows), F32),
            pltpu.VMEM((1, rows), jnp.int32),
            pltpu.VMEM((1, rows), jnp.int32),
            pltpu.VMEM((2, KEY_BLOCK, item_rows), F32),
            pltpu.VMEM((2, KEY_BLOCK, item_rows), F32),
            pltpu.SMEM((3, pairs + 4), jnp.int32),
            pltpu.SemaphoreType.DMA((2 * len(sources),)),
        ],
        compiler_params=pltpu.CompilerParams(vmem_limit_bytes=40 << 20),
        cost_estimate=pl.CostEstimate(
            flops=10 * total * rows * size // 2,
            bytes_accessed=4 * rows * size + 8 * total * size,
            transcendentals=total * rows // 2,
        ),
    )(*operands)


def shift(value, steps):
    count = lax.axis_size("ctx")
    first, last = max(0, -steps), min(count, count - steps)
    return lax.ppermute(value, "ctx", [(s, s + steps) for s in range(first, last)])


def with_reach(reach, tokens, group, scalars, q, do, lse, delta, kv):
    heads = kv.shape[0]
    size = kv.shape[3]
    parts = lax.axis_size("head")
    far = []
    distance = 1
    while reach > 0 and distance < lax.axis_size("ctx"):
        length = min(reach, tokens)
        far.append((distance, tokens - length, length))
        reach -= length
        distance += 1
    arrived = [
        [shift(kv[h][:, offset:], distance) for distance, offset, _ in far] for h in range(heads)
    ]
    query_parts, key_parts = [], []
    for h in range(heads):
        sources = [(0, 0, tokens)] + far
        dq, own, *sent = attend(
            sources, tokens, group, scalars, q[h], do[h], lse[h], delta[h],
            [kv[h], *arrived[h]], None, True,
        )
        query_parts.append(
            lax.all_to_all(dq, "head", split_axis=0, concat_axis=0, tiled=True)
        )
        total = own
        for (distance, offset, _), part in zip(far, sent):
            back = shift(part, -distance).astype(F32)
            total = total + jnp.pad(back, ((0, 0), (offset, 0), (0, 0)))
        total = total.astype(BF16).reshape(2, parts, tokens // parts, size).transpose(1, 0, 2, 3)
        key_parts.append(lax.all_to_all(total, "head", split_axis=0, concat_axis=0, tiled=True))
    mine = tokens // parts
    dq = jnp.stack(query_parts).reshape(
        heads, parts, mine // QUERY_BLOCK, group, QUERY_BLOCK, size
    )
    dq = dq.transpose(2, 4, 1, 0, 3, 5).reshape(mine, parts * heads * group, size)
    dkv = jnp.stack(key_parts)
    dkv = dkv.transpose(2, 3, 1, 0, 4).reshape(2, mine, parts * heads, size)
    return dq, dkv[0], dkv[1]


def shards(query, keys, values, attn_out, output_gradient, lse, doc_offsets, tile_first):
    tokens, local_heads, size = query.shape
    heads = keys.shape[1]
    group = local_heads // heads
    blocks = tokens // QUERY_BLOCK
    count = lax.axis_size("ctx")
    shard = lax.axis_index("ctx")

    def by_head(value):
        value = value.reshape(blocks, QUERY_BLOCK, heads, group, size)
        return value.transpose(2, 0, 3, 1, 4).reshape(heads, blocks * group * QUERY_BLOCK, size)

    delta = jnp.sum(output_gradient.astype(F32) * attn_out.astype(F32), axis=-1)
    delta = delta.reshape(blocks, QUERY_BLOCK, heads, group).transpose(2, 0, 3, 1)
    delta = delta.reshape(heads, 1, -1)
    lse = (lse * LOG2E).reshape(heads, group, blocks, QUERY_BLOCK).transpose(0, 2, 1, 3)
    lse = lse.reshape(heads, 1, -1)
    kv = jnp.stack([keys.transpose(1, 0, 2), values.transpose(1, 0, 2)], axis=1)
    scalars = (doc_offsets, tile_first, shard.reshape(1))
    args = (scalars, by_head(query), by_head(output_gradient), lse, delta, kv)

    reach = jnp.max(jnp.arange(count, dtype=jnp.int32) * tokens - tile_first * TILE)
    longest = min(-(-(LOOKBACK_TOKENS - 1) // TILE) * TILE, (count - 1) * tokens)
    limits = [length for length in range(2 * BUCKET, longest + 1, BUCKET)]
    branches = [
        functools.partial(with_reach, limit, tokens, group) for limit in limits
    ]
    index = jnp.sum((reach > jnp.array(limits[:-1])).astype(jnp.int32))
    return lax.switch(index, branches, *args)


def solution(mesh):
    in_specs = (
        P("ctx", "head", None),
        P("ctx", "head", None),
        P("ctx", "head", None),
        P("ctx", "head", None),
        P("ctx", "head", None),
        P("head", "ctx"),
        P(),
        P(),
    )
    out_specs = (
        P(("ctx", "head"), None, None),
        P(("ctx", "head"), None, None),
        P(("ctx", "head"), None, None),
    )
    return jax.shard_map(shards, mesh=mesh, in_specs=in_specs, out_specs=out_specs, check_vma=False)
```

```python
import functools
import math

import jax
import jax.numpy as jnp
from jax import lax
from jax.experimental import pallas as pl
from jax.experimental.pallas import tpu as pltpu
from jax.sharding import PartitionSpec as P

LOOKBACK_TOKENS = 4096
TILE = 128
QUERY_BLOCK = 128
KEY_BLOCK = 256
BUCKET = 1024
VMEM_LIMIT = 60 << 20
F32 = jnp.float32
BF16 = jnp.bfloat16
LOG2E = math.log2(math.e)


def dot(a, b, dim_a, dim_b):
    return lax.dot_general(
        a, b, (((dim_a,), (dim_b,)), ((), ())), preferred_element_type=F32
    )


def lower_bound(positions, offsets_ref, floor):
    bound = jnp.maximum(positions - (LOOKBACK_TOKENS - 1), floor)
    for d in range(1, offsets_ref.shape[0] - 1):
        cut = offsets_ref[d]
        bound = jnp.where(positions >= cut, jnp.maximum(bound, cut), bound)
    return bound


def each(count, body):
    def step(index, carry):
        body(index)
        return carry

    lax.fori_loop(0, count, step, 0)


def attention_kernel(
    heads, sources, tokens, group, has_partial, last,
    offsets_ref, first_ref, place_ref, q_hbm, do_hbm, lse_ref, delta_ref, *rest
):
    count = len(sources)
    kv_refs, rest = rest[:count], rest[count:]
    if has_partial:
        partial_hbm, rest = rest[0], rest[1:]
    dq_out, rest = rest[0], rest[1:]
    dkv_refs, rest = rest[:count], rest[count:]
    if has_partial:
        before, rest = rest[0], rest[1:]
    (q_ref, do_ref, k_all, v_all, kt_all, dk_acc, dv_acc, dq_acc, lse_rows, delta_rows,
     lo_rows, pos_rows, scores, dprobs, work, sems) = rest
    item_rows = group * QUERY_BLOCK
    blocks = tokens // QUERY_BLOCK
    head_rows = blocks * item_rows
    size = q_ref.shape[1]
    scale = LOG2E / math.sqrt(size)
    shard = place_ref[0]
    query_start = shard * tokens
    floor = first_ref[shard] * TILE

    copies = []

    def fetch(source, target):
        copy = pltpu.make_async_copy(source, target, sems.at[len(copies)])
        copy.start()
        copies.append(copy)
        return copy

    starts = {}
    total = 0
    key_copies = []
    for slot, h in enumerate(heads):
        for index, (_, _, length) in enumerate(sources):
            starts[slot, index] = total
            at = pl.ds(total, length)
            lead = h % kv_refs[index].shape[0]
            key_copies.append(fetch(kv_refs[index].at[lead, 0], k_all.at[at]))
            total += length
    query_copies = []
    for slot, h in enumerate(heads):
        at = pl.ds(slot * head_rows, head_rows)
        query_copies.append(fetch(q_hbm.at[h], q_ref.at[at]))
        query_copies.append(fetch(do_hbm.at[h], do_ref.at[at]))
        for index, (_, _, length) in enumerate(sources):
            at = pl.ds(starts[slot, index], length)
            lead = h % kv_refs[index].shape[0]
            query_copies.append(fetch(kv_refs[index].at[lead, 1], v_all.at[at]))
    partial_copies = []
    if has_partial:
        for slot, h in enumerate(heads):
            at = pl.ds(slot * head_rows, head_rows)
            source = partial_hbm.at[:, pl.ds(h * head_rows, head_rows)]
            partial_copies.append(fetch(source, before.at[:, at]))

    def clear(ik):
        at = pl.ds(pl.multiple_of(ik * KEY_BLOCK, KEY_BLOCK), KEY_BLOCK)
        dk_acc[at, :] = jnp.zeros((KEY_BLOCK, size), F32)
        dv_acc[at, :] = jnp.zeros((KEY_BLOCK, size), F32)

    each(total // KEY_BLOCK, clear)

    def clear_dq(b):
        at = pl.ds(pl.multiple_of(b * item_rows, item_rows), item_rows)
        dq_acc[:, at] = jnp.zeros((size, item_rows), F32)

    each(len(heads) * blocks, clear_dq)

    bounds = [
        lower_bound(query_start + b * QUERY_BLOCK, offsets_ref, floor) for b in range(blocks)
    ]
    lane = lax.broadcasted_iota(jnp.int32, (1, QUERY_BLOCK), 1)

    def fill_rows(b):
        positions = lane + (query_start + b * QUERY_BLOCK)
        bound = lower_bound(positions, offsets_ref, floor)
        for g in range(group):
            at = pl.ds(pl.multiple_of(b * item_rows + g * QUERY_BLOCK, QUERY_BLOCK), QUERY_BLOCK)
            lo_rows[:, at] = bound
            pos_rows[:, at] = positions
            for slot, h in enumerate(heads):
                row = pl.multiple_of(
                    slot * head_rows + b * item_rows + g * QUERY_BLOCK, QUERY_BLOCK
                )
                here = pl.ds(row, QUERY_BLOCK)
                there = pl.ds(pl.multiple_of(b * QUERY_BLOCK, QUERY_BLOCK), QUERY_BLOCK)
                line = h * group + g
                lse_rows[:, here] = lse_ref[line : line + 1, there] * LOG2E
                delta_rows[:, here] = delta_ref[line : line + 1, there]

    each(blocks, fill_rows)

    filled = jnp.int32(0)
    for index, (distance, offset, length) in enumerate(sources):
        base = (shard - distance) * tokens + offset
        skip = jnp.clip((bounds[0] - base) // KEY_BLOCK, 0, length // KEY_BLOCK)
        for slot in range(len(heads)):
            start = starts[slot, index]

            def add_key_block(ik, filled, base=base, start=start, slot=slot):
                key_start = base + ik * KEY_BLOCK
                for b in range(blocks):
                    active = (key_start + (KEY_BLOCK - 1) >= bounds[b]) & (
                        key_start <= query_start + (b * QUERY_BLOCK + QUERY_BLOCK - 1)
                    )
                    work[0, filled] = start + ik * KEY_BLOCK
                    work[1, filled] = slot * head_rows + b * item_rows
                    work[2, filled] = b * item_rows
                    work[3, filled] = key_start
                    filled = filled + active.astype(jnp.int32)
                return filled

            filled = lax.fori_loop(skip, length // KEY_BLOCK, add_key_block, filled)
    for extra in range(2):
        work[0, filled + extra] = 0
        work[1, filled + extra] = 0
        work[2, filled + extra] = 0
        work[3, filled + extra] = jnp.int32(1 << 30)

    for copy in key_copies:
        copy.wait()

    def turn(ik):
        at = pl.ds(pl.multiple_of(ik * KEY_BLOCK, KEY_BLOCK), KEY_BLOCK)
        kt_all[:, at] = k_all[at, :].T

    each(total // KEY_BLOCK, turn)
    for copy in query_copies:
        copy.wait()

    def place(item):
        key_rows = pl.ds(pl.multiple_of(work[0, item], KEY_BLOCK), KEY_BLOCK)
        query_rows = pl.ds(pl.multiple_of(work[1, item], item_rows), item_rows)
        return key_rows, query_rows

    def products(item, slot):
        key_rows, query_rows = place(item)
        scores[slot] = dot(k_all[key_rows, :], q_ref[query_rows, :], 1, 1)
        dprobs[slot] = dot(v_all[key_rows, :], do_ref[query_rows, :], 1, 1)

    def gradients(item, slot):
        key_rows, query_rows = place(item)
        mask_rows = pl.ds(pl.multiple_of(work[2, item], item_rows), item_rows)
        keys = lax.broadcasted_iota(jnp.int32, (KEY_BLOCK, 1), 0) + work[3, item]
        seen = (keys >= lo_rows[:, mask_rows]) & (keys <= pos_rows[:, mask_rows])
        probs = jnp.where(
            seen, jnp.exp2(scores[slot] * scale - lse_rows[:, query_rows]), 0.0
        )
        dv_acc[key_rows, :] += dot(probs.astype(BF16), do_ref[query_rows, :], 1, 0)
        dscores = (probs * (dprobs[slot] - delta_rows[:, query_rows])).astype(BF16)
        dk_acc[key_rows, :] += dot(dscores, q_ref[query_rows, :], 1, 0)
        dq_acc[:, query_rows] += dot(kt_all[:, key_rows], dscores, 1, 0)

    @pl.when(filled > 0)
    def _():
        products(0, 0)

        def two_items(step):
            item = 2 * step
            products(item + 1, 1)
            gradients(item, 0)
            products(item + 2, 0)
            gradients(item + 1, 1)

        each((filled + 1) // 2, two_items)

    out_scale = 1.0 / math.sqrt(size)
    for slot in range(len(heads)):
        for index, (_, _, length) in enumerate(sources):

            def write(ik, slot=slot, index=index):
                to = pl.ds(pl.multiple_of(ik * KEY_BLOCK, KEY_BLOCK), KEY_BLOCK)
                at = pl.multiple_of(starts[slot, index] + ik * KEY_BLOCK, KEY_BLOCK)
                at = pl.ds(at, KEY_BLOCK)
                out = dkv_refs[index]
                out[slot, 0, to, :] = (dk_acc[at, :] * out_scale).astype(out.dtype)
                out[slot, 1, to, :] = dv_acc[at, :].astype(out.dtype)

            each(length // KEY_BLOCK, write)
    for copy in partial_copies:
        copy.wait()

    def dq_block(at):
        return dq_acc[:, at] + before[:, at] if has_partial else dq_acc[:, at]

    if last:

        def write_dq(b):
            at = pl.ds(pl.multiple_of(b * item_rows, item_rows), item_rows)
            dq_out[at, :] = (dq_block(at).T * out_scale).astype(BF16)

        each(len(heads) * blocks, write_dq)
    else:

        def keep_dq(b):
            at = pl.ds(pl.multiple_of(b * item_rows, item_rows), item_rows)
            dq_out[:, at] = dq_block(at)

        each(len(heads) * blocks, keep_dq)


def attend(heads, sources, tokens, group, scalars, q, do, lse, delta, kvs, partial, last):
    rows, size = q.shape[1:]
    total = sum(length for _, _, length in sources) * len(heads)
    all_rows = rows * len(heads)
    any_space = pl.BlockSpec(memory_space=pl.ANY)
    vmem = pl.BlockSpec(memory_space=pltpu.VMEM)
    smem = pl.BlockSpec(memory_space=pltpu.SMEM)
    operands = [*scalars, q, do, lse, delta, *kvs]
    specs = [smem] * 3 + [any_space] * 2 + [vmem] * 2 + [any_space] * len(kvs)
    if partial is not None:
        operands.append(partial)
        specs.append(any_space)
    dq_shape = (
        jax.ShapeDtypeStruct((all_rows, size), BF16)
        if last
        else jax.ShapeDtypeStruct((size, all_rows), F32)
    )
    dkv_shapes = [
        jax.ShapeDtypeStruct((len(heads), 2, length, size), F32 if distance == 0 else BF16)
        for distance, _, length in sources
    ]
    item_rows = group * QUERY_BLOCK
    pairs = (total // KEY_BLOCK) * (tokens // QUERY_BLOCK)
    out = pl.pallas_call(
        functools.partial(
            attention_kernel, heads, sources, tokens, group, partial is not None, last
        ),
        out_shape=[dq_shape] + dkv_shapes,
        in_specs=specs,
        out_specs=[vmem] * (1 + len(dkv_shapes)),
        scratch_shapes=[pltpu.VMEM((size, all_rows), F32)] * (partial is not None)
        + [
            pltpu.VMEM((all_rows, size), BF16),
            pltpu.VMEM((all_rows, size), BF16),
            pltpu.VMEM((total, size), BF16),
            pltpu.VMEM((total, size), BF16),
            pltpu.VMEM((size, total), BF16),
            pltpu.VMEM((total, size), F32),
            pltpu.VMEM((total, size), F32),
            pltpu.VMEM((size, all_rows), F32),
            pltpu.VMEM((1, all_rows), F32),
            pltpu.VMEM((1, all_rows), F32),
            pltpu.VMEM((1, rows), jnp.int32),
            pltpu.VMEM((1, rows), jnp.int32),
            pltpu.VMEM((2, KEY_BLOCK, item_rows), F32),
            pltpu.VMEM((2, KEY_BLOCK, item_rows), F32),
            pltpu.SMEM((4, pairs + 4), jnp.int32),
            pltpu.SemaphoreType.DMA((len(heads) * (2 * len(sources) + 3),)),
        ],
        compiler_params=pltpu.CompilerParams(vmem_limit_bytes=VMEM_LIMIT),
        cost_estimate=pl.CostEstimate(
            flops=10 * total * rows * size // 2,
            bytes_accessed=4 * all_rows * size + 8 * total * size,
            transcendentals=total * rows // 2,
        ),
    )(*operands)
    return out[0], out[1:]


def interleave_kernel(pieces, *refs):
    inputs, outputs, wide = refs[: -len(pieces) - 1], refs[-len(pieces) - 1 : -1], refs[-1]
    for out, listed in zip(outputs, pieces):
        mine, all_heads, size = out.shape
        for index, lead, column, columns in listed:
            view = inputs[index].at[lead]
            token_blocks, _, span, _ = view.shape

            def spread(i, view=view, column=column, columns=columns, span=span):
                b = i // columns
                c = lax.rem(i, columns)
                to = pl.ds(b * span * all_heads + column + c, span, stride=all_heads)
                wide[to, :] = view[b, c].astype(F32)

            each(token_blocks * columns, spread)

        def write(b, out=out, all_heads=all_heads):
            at = pl.ds(pl.multiple_of(b * 16, 16), 16)
            from_rows = pl.ds(pl.multiple_of(b * 16 * all_heads, 16 * all_heads), 16 * all_heads)
            out[at] = wide[from_rows, :].astype(BF16).reshape(16, all_heads, size)

        each(mine // 16, write)


def interleave(pieces, arrays, mine, size, columns):
    vmem = pl.BlockSpec(memory_space=pltpu.VMEM)
    return pl.pallas_call(
        functools.partial(interleave_kernel, pieces),
        out_shape=[jax.ShapeDtypeStruct((mine, columns, size), BF16)] * len(pieces),
        in_specs=[vmem] * len(arrays),
        out_specs=[vmem] * len(pieces),
        scratch_shapes=[pltpu.VMEM((mine * columns, size), F32)],
        compiler_params=pltpu.CompilerParams(vmem_limit_bytes=32 << 20),
        cost_estimate=pl.CostEstimate(
            flops=0, bytes_accessed=4 * len(pieces) * mine * columns * size, transcendentals=0
        ),
    )(*arrays)


def shift(value, steps):
    count = lax.axis_size("ctx")
    first, last = max(0, -steps), min(count, count - steps)
    return lax.ppermute(value, "ctx", [(s, s + steps) for s in range(first, last)])


def to_parts(value):
    return lax.all_to_all(value, "head", split_axis=0, concat_axis=0, tiled=True)


def with_reach(reach, scalars, query, keys, values, attn_out, output_gradient, lse):
    tokens, local_heads, size = query.shape
    heads = keys.shape[1]
    group = local_heads // heads
    blocks = tokens // QUERY_BLOCK
    parts = lax.axis_size("head")
    far = []
    distance = 1
    while reach > 0 and distance < lax.axis_size("ctx"):
        length = min(reach, tokens)
        far.append((distance, tokens - length, length))
        reach -= length
        distance += 1

    kv = jnp.stack([keys.transpose(1, 0, 2), values.transpose(1, 0, 2)], axis=1)
    arrived = []
    for h in range(heads):
        own_kv = kv[h : h + 1]
        if arrived:
            own_kv = lax.optimization_barrier((own_kv, arrived[-1]))[0]
        got = []
        for distance, offset, _ in far:
            got.append(shift(own_kv[:, :, offset:], distance))
        arrived.append(got)

    def by_head(value):
        value = value.reshape(blocks, QUERY_BLOCK, heads, group, size)
        return value.transpose(2, 0, 3, 1, 4).reshape(heads, blocks * group * QUERY_BLOCK, size)

    delta = jnp.sum(output_gradient.astype(F32) * attn_out.astype(F32), axis=-1)
    delta = delta.T
    q, do = by_head(query), by_head(output_gradient)

    partial, (own,) = attend(
        tuple(range(heads)), [(0, 0, tokens)], tokens, group, scalars, q, do, lse, delta,
        [kv], None, False,
    )
    mine = tokens // parts
    query_parts, key_parts, backs = [], [], []
    for h in range(heads):
        dq, sent = attend(
            (h,), far, tokens, group, scalars, q, do, lse, delta, arrived[h], partial, True
        )
        query_parts.append(to_parts(dq).reshape(parts, -1, group, QUERY_BLOCK, size))
        backs.append(
            [shift(part, -distance) for (distance, _, _), part in zip(far, sent)]
        )
    listed = [
        [(h, part, (part * heads + h) * group, group) for h in range(heads) for part in range(parts)]
    ]
    (dq,) = interleave(listed, query_parts, mine, size, parts * local_heads)
    for h in range(heads):
        back = backs[h]
        if h == heads - 1:
            back, dq, key_parts = lax.optimization_barrier((back, dq, key_parts))
        total = own[h]
        for (_, offset, _), part in zip(far, back):
            total = total + jnp.pad(part[0].astype(F32), ((0, 0), (offset, 0), (0, 0)))
        total = total.astype(BF16).reshape(2, parts, mine, size).transpose(1, 0, 2, 3)
        key_parts = key_parts + [to_parts(total).reshape(parts, 2, 1, 1, mine, size)]
    listed = [
        [(h, (part, o), part * heads + h, 1) for h in range(heads) for part in range(parts)]
        for o in range(2)
    ]
    dk, dv = interleave(listed, key_parts, mine, size, parts * heads)
    return dq, dk, dv


def shards(query, keys, values, attn_out, output_gradient, lse, doc_offsets, tile_first):
    tokens = query.shape[0]
    count = lax.axis_size("ctx")
    place = jnp.stack([lax.axis_index("ctx"), lax.axis_index("head")]).astype(jnp.int32)
    scalars = (doc_offsets, tile_first, place)
    reach = jnp.max(jnp.arange(count, dtype=jnp.int32) * tokens - tile_first * TILE)
    longest = min(-(-(LOOKBACK_TOKENS - 1) // TILE) * TILE, (count - 1) * tokens)
    limits = [length for length in range(2 * BUCKET, longest + 1, BUCKET)]
    branches = [functools.partial(with_reach, limit) for limit in limits]
    index = sum(((reach > limit).astype(jnp.int32) for limit in limits[:-1]), jnp.int32(0))
    return lax.switch(
        index, branches, scalars, query, keys, values, attn_out, output_gradient, lse
    )


def solution(mesh):
    in_specs = (
        P("ctx", "head", None),
        P("ctx", "head", None),
        P("ctx", "head", None),
        P("ctx", "head", None),
        P("ctx", "head", None),
        P("head", "ctx"),
        P(),
        P(),
    )
    out_specs = (
        P(("ctx", "head"), None, None),
        P(("ctx", "head"), None, None),
        P(("ctx", "head"), None, None),
    )
    return jax.shard_map(shards, mesh=mesh, in_specs=in_specs, out_specs=out_specs, check_vma=False)
```

```python
import functools
import math

import jax
import jax.numpy as jnp
from jax import lax
from jax.experimental import pallas as pl
from jax.experimental.pallas import tpu as pltpu
from jax.sharding import PartitionSpec as P

LOOKBACK_TOKENS = 4096
TILE = 128
QUERY_BLOCK = 128
KEY_BLOCK = 256
BUCKET = 1024
VMEM_LIMIT = 60 << 20
INTERLEAVE_TOKENS = 32
F32 = jnp.float32
BF16 = jnp.bfloat16
LOG2E = math.log2(math.e)


def dot(a, b, dim_a, dim_b):
    return lax.dot_general(
        a, b, (((dim_a,), (dim_b,)), ((), ())), preferred_element_type=F32
    )


def lower_bound(positions, offsets_ref, floor):
    bound = jnp.maximum(positions - (LOOKBACK_TOKENS - 1), floor)
    for d in range(1, offsets_ref.shape[0] - 1):
        cut = offsets_ref[d]
        bound = jnp.where(positions >= cut, jnp.maximum(bound, cut), bound)
    return bound


def each(count, body):
    def step(index, carry):
        body(index)
        return carry

    lax.fori_loop(0, count, step, 0)


def attention_kernel(
    heads, sources, tokens, group, has_partial, last,
    offsets_ref, first_ref, place_ref, q_hbm, do_hbm, lse_ref, delta_ref, *rest
):
    count = len(sources)
    kv_refs, rest = rest[:count], rest[count:]
    if has_partial:
        partial_hbm, rest = rest[0], rest[1:]
    dq_out, rest = rest[0], rest[1:]
    dkv_refs, rest = rest[:count], rest[count:]
    if has_partial:
        before, rest = rest[0], rest[1:]
    if last:
        (dq_rows, k_out, v_out), rest = rest[:3], rest[3:]
    (q_ref, do_ref, k_all, v_all, kt_all, dk_acc, dv_acc, dq_acc, lse_rows, delta_rows,
     lo_rows, pos_rows, scores, dprobs, work, sems) = rest
    item_rows = group * QUERY_BLOCK
    blocks = tokens // QUERY_BLOCK
    head_rows = blocks * item_rows
    size = q_ref.shape[1]
    scale = LOG2E / math.sqrt(size)
    shard = place_ref[0]
    query_start = shard * tokens
    floor = first_ref[shard] * TILE

    copies = []

    def fetch(source, target):
        copy = pltpu.make_async_copy(source, target, sems.at[len(copies)])
        copy.start()
        copies.append(copy)
        return copy

    starts = {}
    total = 0
    key_copies = []
    for slot, h in enumerate(heads):
        for index, (_, _, length) in enumerate(sources):
            starts[slot, index] = total
            at = pl.ds(total, length)
            lead = h % kv_refs[index].shape[0]
            key_copies.append(fetch(kv_refs[index].at[lead, 0], k_all.at[at]))
            total += length
    query_copies = []
    for slot, h in enumerate(heads):
        at = pl.ds(slot * head_rows, head_rows)
        query_copies.append(fetch(q_hbm.at[h], q_ref.at[at]))
        query_copies.append(fetch(do_hbm.at[h], do_ref.at[at]))
        for index, (_, _, length) in enumerate(sources):
            at = pl.ds(starts[slot, index], length)
            lead = h % kv_refs[index].shape[0]
            query_copies.append(fetch(kv_refs[index].at[lead, 1], v_all.at[at]))
    partial_copies = []
    if has_partial:
        for slot, h in enumerate(heads):
            at = pl.ds(slot * head_rows, head_rows)
            source = partial_hbm.at[:, pl.ds(h * head_rows, head_rows)]
            partial_copies.append(fetch(source, before.at[:, at]))

    def clear(ik):
        at = pl.ds(pl.multiple_of(ik * KEY_BLOCK, KEY_BLOCK), KEY_BLOCK)
        dk_acc[at, :] = jnp.zeros((KEY_BLOCK, size), F32)
        dv_acc[at, :] = jnp.zeros((KEY_BLOCK, size), F32)

    each(total // KEY_BLOCK, clear)

    def clear_dq(b):
        at = pl.ds(pl.multiple_of(b * item_rows, item_rows), item_rows)
        dq_acc[:, at] = jnp.zeros((size, item_rows), F32)

    each(len(heads) * blocks, clear_dq)

    bounds = [
        lower_bound(query_start + b * QUERY_BLOCK, offsets_ref, floor) for b in range(blocks)
    ]
    lane = lax.broadcasted_iota(jnp.int32, (1, QUERY_BLOCK), 1)

    def fill_rows(b):
        positions = lane + (query_start + b * QUERY_BLOCK)
        bound = lower_bound(positions, offsets_ref, floor)
        for g in range(group):
            at = pl.ds(pl.multiple_of(b * item_rows + g * QUERY_BLOCK, QUERY_BLOCK), QUERY_BLOCK)
            lo_rows[:, at] = bound
            pos_rows[:, at] = positions
            for slot, h in enumerate(heads):
                row = pl.multiple_of(
                    slot * head_rows + b * item_rows + g * QUERY_BLOCK, QUERY_BLOCK
                )
                here = pl.ds(row, QUERY_BLOCK)
                there = pl.ds(pl.multiple_of(b * QUERY_BLOCK, QUERY_BLOCK), QUERY_BLOCK)
                line = h * group + g
                lse_rows[:, here] = lse_ref[line : line + 1, there] * LOG2E
                delta_rows[:, here] = delta_ref[line : line + 1, there]

    each(blocks, fill_rows)

    filled = jnp.int32(0)
    for index, (distance, offset, length) in enumerate(sources):
        base = (shard - distance) * tokens + offset
        skip = jnp.clip((bounds[0] - base) // KEY_BLOCK, 0, length // KEY_BLOCK)
        for slot in range(len(heads)):
            start = starts[slot, index]

            def add_key_block(ik, filled, base=base, start=start, slot=slot):
                key_start = base + ik * KEY_BLOCK
                for b in range(blocks):
                    active = (key_start + (KEY_BLOCK - 1) >= bounds[b]) & (
                        key_start <= query_start + (b * QUERY_BLOCK + QUERY_BLOCK - 1)
                    )
                    work[0, filled] = start + ik * KEY_BLOCK
                    work[1, filled] = slot * head_rows + b * item_rows
                    work[2, filled] = b * item_rows
                    work[3, filled] = key_start
                    filled = filled + active.astype(jnp.int32)
                return filled

            filled = lax.fori_loop(skip, length // KEY_BLOCK, add_key_block, filled)
    for extra in range(2):
        work[0, filled + extra] = 0
        work[1, filled + extra] = 0
        work[2, filled + extra] = 0
        work[3, filled + extra] = jnp.int32(1 << 30)

    for copy in key_copies:
        copy.wait()

    def turn(ik):
        at = pl.ds(pl.multiple_of(ik * KEY_BLOCK, KEY_BLOCK), KEY_BLOCK)
        kt_all[:, at] = k_all[at, :].T

    each(total // KEY_BLOCK, turn)
    for copy in query_copies:
        copy.wait()

    def place(item):
        key_rows = pl.ds(pl.multiple_of(work[0, item], KEY_BLOCK), KEY_BLOCK)
        query_rows = pl.ds(pl.multiple_of(work[1, item], item_rows), item_rows)
        return key_rows, query_rows

    def products(item, slot):
        key_rows, query_rows = place(item)
        scores[slot] = dot(k_all[key_rows, :], q_ref[query_rows, :], 1, 1)
        dprobs[slot] = dot(v_all[key_rows, :], do_ref[query_rows, :], 1, 1)

    def gradients(item, slot):
        key_rows, query_rows = place(item)
        mask_rows = pl.ds(pl.multiple_of(work[2, item], item_rows), item_rows)
        keys = lax.broadcasted_iota(jnp.int32, (KEY_BLOCK, 1), 0) + work[3, item]
        seen = (keys >= lo_rows[:, mask_rows]) & (keys <= pos_rows[:, mask_rows])
        probs = jnp.where(
            seen, jnp.exp2(scores[slot] * scale - lse_rows[:, query_rows]), 0.0
        )
        dv_acc[key_rows, :] += dot(probs.astype(BF16), do_ref[query_rows, :], 1, 0)
        dscores = (probs * (dprobs[slot] - delta_rows[:, query_rows])).astype(BF16)
        dk_acc[key_rows, :] += dot(dscores, q_ref[query_rows, :], 1, 0)
        dq_acc[:, query_rows] += dot(kt_all[:, key_rows], dscores, 1, 0)

    @pl.when(filled > 0)
    def _():
        products(0, 0)

        def two_items(step):
            item = 2 * step
            products(item + 1, 1)
            gradients(item, 0)
            products(item + 2, 0)
            gradients(item + 1, 1)

        each((filled + 1) // 2, two_items)

    out_scale = 1.0 / math.sqrt(size)
    leaving = []

    def send(source, target):
        copy = pltpu.make_async_copy(source, target, sems.at[len(copies) + len(leaving)])
        copy.start()
        leaving.append(copy)

    for slot in range(len(heads)):
        for index, (_, _, length) in enumerate(sources):
            start = starts[slot, index]
            at = pl.ds(start, length)

            def finish(ik, start=start):
                at = pl.ds(pl.multiple_of(start + ik * KEY_BLOCK, KEY_BLOCK), KEY_BLOCK)
                if last:
                    k_out[at, :] = (dk_acc[at, :] * out_scale).astype(BF16)
                    v_out[at, :] = dv_acc[at, :].astype(BF16)
                else:
                    dk_acc[at, :] = dk_acc[at, :] * out_scale

            each(length // KEY_BLOCK, finish)
            send((k_out if last else dk_acc).at[at], dkv_refs[index].at[slot, 0])
            send((v_out if last else dv_acc).at[at], dkv_refs[index].at[slot, 1])
    for copy in partial_copies:
        copy.wait()
    if last:
        half = head_rows // 2
        for part in range(2 * len(heads)):

            def write_dq(b, part=part):
                row = pl.multiple_of(part * half + b * item_rows, item_rows)
                at = pl.ds(row, item_rows)
                block = dq_acc[:, at]
                if has_partial:
                    block = block + before[:, at]
                dq_rows[at, :] = (block.T * out_scale).astype(BF16)

            each(half // item_rows, write_dq)
            at = pl.ds(part * half, half)
            send(dq_rows.at[at], dq_out.at[at])
    else:
        send(dq_acc, dq_out)
    for copy in leaving:
        copy.wait()


def attend(heads, sources, tokens, group, scalars, q, do, lse, delta, kvs, partial, last):
    rows, size = q.shape[1:]
    total = sum(length for _, _, length in sources) * len(heads)
    all_rows = rows * len(heads)
    any_space = pl.BlockSpec(memory_space=pl.ANY)
    vmem = pl.BlockSpec(memory_space=pltpu.VMEM)
    smem = pl.BlockSpec(memory_space=pltpu.SMEM)
    operands = [*scalars, q, do, lse, delta, *kvs]
    specs = [smem] * 3 + [any_space] * 2 + [vmem] * 2 + [any_space] * len(kvs)
    if partial is not None:
        operands.append(partial)
        specs.append(any_space)
    dq_shape = (
        jax.ShapeDtypeStruct((all_rows, size), BF16)
        if last
        else jax.ShapeDtypeStruct((size, all_rows), F32)
    )
    dkv_shapes = [
        jax.ShapeDtypeStruct((len(heads), 2, length, size), F32 if distance == 0 else BF16)
        for distance, _, length in sources
    ]
    item_rows = group * QUERY_BLOCK
    pairs = (total // KEY_BLOCK) * (tokens // QUERY_BLOCK)
    out = pl.pallas_call(
        functools.partial(
            attention_kernel, heads, sources, tokens, group, partial is not None, last
        ),
        out_shape=[dq_shape] + dkv_shapes,
        in_specs=specs,
        out_specs=[any_space] * (1 + len(dkv_shapes)),
        scratch_shapes=[pltpu.VMEM((size, all_rows), F32)] * (partial is not None)
        + [
            pltpu.VMEM((all_rows, size), BF16),
            pltpu.VMEM((total, size), BF16),
            pltpu.VMEM((total, size), BF16),
        ]
        * last
        + [
            pltpu.VMEM((all_rows, size), BF16),
            pltpu.VMEM((all_rows, size), BF16),
            pltpu.VMEM((total, size), BF16),
            pltpu.VMEM((total, size), BF16),
            pltpu.VMEM((size, total), BF16),
            pltpu.VMEM((total, size), F32),
            pltpu.VMEM((total, size), F32),
            pltpu.VMEM((size, all_rows), F32),
            pltpu.VMEM((1, all_rows), F32),
            pltpu.VMEM((1, all_rows), F32),
            pltpu.VMEM((1, rows), jnp.int32),
            pltpu.VMEM((1, rows), jnp.int32),
            pltpu.VMEM((2, KEY_BLOCK, item_rows), F32),
            pltpu.VMEM((2, KEY_BLOCK, item_rows), F32),
            pltpu.SMEM((4, pairs + 4), jnp.int32),
            pltpu.SemaphoreType.DMA((len(heads) * (4 * len(sources) + 5),)),
        ],
        compiler_params=pltpu.CompilerParams(vmem_limit_bytes=VMEM_LIMIT),
        cost_estimate=pl.CostEstimate(
            flops=10 * total * rows * size // 2,
            bytes_accessed=4 * all_rows * size + 8 * total * size,
            transcendentals=total * rows // 2,
        ),
    )(*operands)
    return out[0], out[1:]


def interleave_kernel(columns, *refs):
    inputs, outputs = refs[: -len(columns)], refs[-len(columns) :]
    for out, listed in zip(outputs, columns):
        span = inputs[listed[0][0]].shape[-2]
        per_block = span // INTERLEAVE_TOKENS

        def write(i, out=out, listed=listed, per_block=per_block):
            b = i // per_block
            t = lax.rem(i, per_block)
            at = pl.ds(pl.multiple_of(t * INTERLEAVE_TOKENS, INTERLEAVE_TOKENS), INTERLEAVE_TOKENS)
            to = pl.ds(pl.multiple_of(i * INTERLEAVE_TOKENS, INTERLEAVE_TOKENS), INTERLEAVE_TOKENS)
            for first in range(0, len(listed), 8):
                rows = [
                    inputs[index].at[lead][b, head, at, :]
                    for index, lead, head in listed[first : first + 8]
                ]
                out[to, first : first + len(rows), :] = jnp.swapaxes(jnp.stack(rows), 0, 1)

        each(out.shape[0] // INTERLEAVE_TOKENS, write)


def interleave(columns, arrays, mine, size):
    vmem = pl.BlockSpec(memory_space=pltpu.VMEM)
    return pl.pallas_call(
        functools.partial(interleave_kernel, columns),
        out_shape=[jax.ShapeDtypeStruct((mine, len(c), size), BF16) for c in columns],
        in_specs=[vmem] * len(arrays),
        out_specs=[vmem] * len(columns),
        compiler_params=pltpu.CompilerParams(vmem_limit_bytes=32 << 20),
        cost_estimate=pl.CostEstimate(
            flops=0,
            bytes_accessed=4 * mine * size * sum(len(c) for c in columns),
            transcendentals=0,
        ),
    )(*arrays)


def shift(value, steps):
    count = lax.axis_size("ctx")
    first, last = max(0, -steps), min(count, count - steps)
    return lax.ppermute(value, "ctx", [(s, s + steps) for s in range(first, last)])


def to_parts(value):
    return lax.all_to_all(value, "head", split_axis=0, concat_axis=0, tiled=True)


def with_reach(reach, scalars, query, keys, values, attn_out, output_gradient, lse):
    tokens, local_heads, size = query.shape
    heads = keys.shape[1]
    group = local_heads // heads
    blocks = tokens // QUERY_BLOCK
    parts = lax.axis_size("head")
    far = []
    distance = 1
    while reach > 0 and distance < lax.axis_size("ctx"):
        length = min(reach, tokens)
        far.append((distance, tokens - length, length))
        reach -= length
        distance += 1

    kv = jnp.stack([keys.transpose(1, 0, 2), values.transpose(1, 0, 2)], axis=1)
    arrived = []
    for h in range(heads):
        own_kv = kv[h : h + 1]
        if arrived:
            own_kv = lax.optimization_barrier((own_kv, arrived[-1]))[0]
        got = []
        for distance, offset, _ in far:
            got.append(shift(own_kv[:, :, offset:], distance))
        arrived.append(got)

    def by_head(value):
        value = value.reshape(blocks, QUERY_BLOCK, heads, group, size)
        return value.transpose(2, 0, 3, 1, 4).reshape(heads, blocks * group * QUERY_BLOCK, size)

    delta = jnp.sum(output_gradient.astype(F32) * attn_out.astype(F32), axis=-1)
    delta = delta.T
    q, do = by_head(query), by_head(output_gradient)

    partial, (own,) = attend(
        tuple(range(heads)), [(0, 0, tokens)], tokens, group, scalars, q, do, lse, delta,
        [kv], None, False,
    )
    mine = tokens // parts
    query_parts, key_parts, backs = [], [], []
    for h in range(heads):
        dq, sent = attend(
            (h,), far, tokens, group, scalars, q, do, lse, delta, arrived[h], partial, True
        )
        query_parts.append(to_parts(dq).reshape(parts, -1, group, QUERY_BLOCK, size))
        backs.append(
            [shift(part, -distance) for (distance, _, _), part in zip(far, sent)]
        )
    columns = [
        (h, part, g) for part in range(parts) for h in range(heads) for g in range(group)
    ]
    (dq,) = interleave([columns], query_parts, mine, size)
    for h in range(heads):
        back = backs[h]
        if h == heads - 1:
            back, dq, key_parts = lax.optimization_barrier((back, dq, key_parts))
        total = own[h]
        for (_, offset, _), part in zip(far, back):
            total = total + jnp.pad(part[0].astype(F32), ((0, 0), (offset, 0), (0, 0)))
        total = total.astype(BF16).reshape(2, parts, mine, size).transpose(1, 0, 2, 3)
        key_parts = key_parts + [to_parts(total).reshape(parts, 2, 1, 1, mine, size)]
    columns = [
        [(h, (part, o), 0) for part in range(parts) for h in range(heads)] for o in range(2)
    ]
    dk, dv = interleave(columns, key_parts, mine, size)
    return dq, dk, dv


def shards(query, keys, values, attn_out, output_gradient, lse, doc_offsets, tile_first):
    tokens = query.shape[0]
    count = lax.axis_size("ctx")
    place = jnp.stack([lax.axis_index("ctx"), lax.axis_index("head")]).astype(jnp.int32)
    scalars = (doc_offsets, tile_first, place)
    reach = jnp.max(jnp.arange(count, dtype=jnp.int32) * tokens - tile_first * TILE)
    longest = min(-(-(LOOKBACK_TOKENS - 1) // TILE) * TILE, (count - 1) * tokens)
    limits = [length for length in range(2 * BUCKET, longest + 1, BUCKET)]
    branches = [functools.partial(with_reach, limit) for limit in limits]
    index = sum(((reach > limit).astype(jnp.int32) for limit in limits[:-1]), jnp.int32(0))
    return lax.switch(
        index, branches, scalars, query, keys, values, attn_out, output_gradient, lse
    )


def solution(mesh):
    in_specs = (
        P("ctx", "head", None),
        P("ctx", "head", None),
        P("ctx", "head", None),
        P("ctx", "head", None),
        P("ctx", "head", None),
        P("head", "ctx"),
        P(),
        P(),
    )
    out_specs = (
        P(("ctx", "head"), None, None),
        P(("ctx", "head"), None, None),
        P(("ctx", "head"), None, None),
    )
    return jax.shard_map(shards, mesh=mesh, in_specs=in_specs, out_specs=out_specs, check_vma=False)
```
